32 devices in a mesh: dp: 2 (over core), row: 4 (over y, x), col: 4 (over z).
Axes of the slice: x: 2, y: 2, z: 4, core: 2. Of those that a mesh axis runs over, the one named last changes fastest.
Arguments:
- inputs: bfloat16 [2, 16, 4, 16, 2048], P('dp', 'row', None, None, 'col'), may hold values from -6 to 6
- up_weight: bfloat16 [2048, 4096], P(None, 'col'), may hold values from -0.1875 to 0.1875
- down_weight: bfloat16 [2048, 4096], P(None, 'col'), may hold values from -0.125 to 0.125
- kernel: float32 [125, 4096], P(None, 'col'), may hold values from -0.625 to 0.625
- cotangent: bfloat16 [2, 16, 4, 16, 2048], P('dp', 'row', None, None, 'col'), may hold values from -2 to 2
Outputs:
- block_output: bfloat16 [2, 16, 4, 16, 2048], P('dp', 'row', None, None, 'col')
- input_grad: bfloat16 [2, 16, 4, 16, 2048], P('dp', 'row', None, None, 'col')
- up_grad: bfloat16 [2048, 4096], P(('dp', 'row'), 'col')
- down_grad: bfloat16 [2048, 4096], P(('dp', 'row'), 'col')
- kernel_grad: float32 [125, 4096], P(None, 'col')
The draws below stay inside these ranges and needn't reach their ends.
All inputs are finite; a program needn't handle non-finite values.
Results may differ from the reference program's by a relative error of at most 0.012.
Values may be sent and summed in bfloat16 or wider, within the bound.
A program may use at most 128 MiB of HBM per device.

```python
import jax
import jax.numpy as jnp
from jax import lax

WIDTH = 2048
EXPAND = 4096
TAPS = 125
STATES_DEV = 1
PLANES = 4
TILE_X = 4
TILE_Y = 16
STATES = 2
DEPTH = 16
N_DP = 2
N_ROW = 4
N_COL = 4


def strengthened(entries, key, source, target, shards_of, factor):
    def block_of(axis_at):
        return (jnp.arange(entries.shape[axis_at]) // (entries.shape[axis_at] // shards_of)).reshape((-1,) + (1,) * (entries.ndim - 1 - axis_at))

    one_side = jax.random.permutation(key, shards_of)[block_of(target)]
    other_side = (block_of(target) + shards_of // 2) % shards_of
    return jnp.where((block_of(source) == one_side) | (block_of(source) == other_side), factor * entries, entries)


def levels(rng, dims, shards, low, largest):
    def one(dim, shards_of):
        heights = jax.random.uniform(jax.random.fold_in(jax.random.fold_in(rng, 6), dim), (shards_of,), jnp.float32, low / len(shards), largest / len(shards))
        return jnp.repeat(jnp.exp(heights), dims[dim] // shards_of).reshape((-1,) + (1,) * (len(dims) - dim - 1))

    level = one(*shards[0])
    for cut in shards[1:]:
        level = level * one(*cut)
    return level


def scatter_about(key, dims, width, bound, cuts=(), kind=jnp.bfloat16):
    array = jax.random.normal(key, dims, jnp.float32) * width
    if len(cuts) > 0:
        array = levels(key, dims, cuts, -0.22, 0.18) * array
    return jnp.clip(array, min=-bound, max=bound).astype(kind)


def gaussian_with(own_key, dims, scale, bound, cuts, heavy, held_as=jnp.bfloat16):
    array = scale * jax.random.normal(own_key, dims, jnp.float32)
    if cuts:
        array = array * levels(own_key, dims, cuts, -0.22, 0.18)
    return jnp.clip(strengthened(array, jax.random.fold_in(own_key, 3), *heavy), -bound, bound).astype(held_as)


def setup_inputs(seed: int = 0) -> dict:
    keys = jax.random.split(jax.random.key(seed), 6)
    return {
        "inputs": scatter_about(keys[0], (STATES, DEPTH, TILE_X, TILE_Y, WIDTH), 1.0, 6.0, ((0, 2), (1, 4), (4, 4))),
        "up_weight": gaussian_with(keys[1], (WIDTH, EXPAND), WIDTH ** -0.5, 0.1875, ((1, 4),), (1, 0, 4, 2.0)),
        "down_weight": gaussian_with(keys[2], (WIDTH, EXPAND), EXPAND ** -0.5, 0.125, ((1, 4),), (1, 0, 4, 2.0)),
        "kernel": scatter_about(keys[3], (TAPS, EXPAND), 0.1, 0.625, ((1, 4),), jnp.float32),
        "cotangent": gaussian_with(keys[4], (STATES, DEPTH, TILE_X, TILE_Y, WIDTH), 0.25, 2.0, ((0, 2), (1, 4), (4, 4)), (1, 4, 4, 2.0)),
    }


def pad_field(field):
    return jnp.pad(field, ((0, 0), (2, 2), (2, 2), (2, 2), (0, 0)))


def stencil_sum(padded, kernel, mirror, planes, tile_x, tile_y):
    result = jnp.zeros(padded.shape[:1] + (planes, tile_x, tile_y, padded.shape[4]), jnp.float32)
    for depth_step in range(5):
        for row_step in range(5):
            for col_step in range(5):
                first_z = depth_step + mirror * (4 - 2 * depth_step)
                first_x = row_step + mirror * (4 - 2 * row_step)
                first_y = col_step + mirror * (4 - 2 * col_step)
                window = padded[:, first_z:first_z + planes, first_x:first_x + tile_x, first_y:first_y + tile_y, :]
                result = result + kernel[25 * depth_step + 5 * row_step + col_step] * window
    return result


def kernel_terms(padded, grad_field, planes, tile_x, tile_y):
    grad_wide = grad_field.astype(jnp.float32)
    rows_list = []
    for depth_step in range(5):
        for row_step in range(5):
            for col_step in range(5):
                window = padded[:, depth_step:depth_step + planes, row_step:row_step + tile_x, col_step:col_step + tile_y, :]
                rows_list.append(jnp.sum(window * grad_wide, axis=(0, 1, 2, 3)))
    return jnp.stack(rows_list)


def rounded(value):
    return lax.optimization_barrier(value.astype(jnp.bfloat16)).astype(jnp.float32)


def block_products(left_rows, weight):
    block_size = weight.shape[1] // N_COL

    def add_block(block_index, running):
        first_col = (block_index * block_size).astype(jnp.int32)
        left_piece = lax.dynamic_slice_in_dim(left_rows, first_col, block_size, 1)
        weight_piece = lax.dynamic_slice_in_dim(weight, first_col, block_size, 1)
        product = jnp.dot(left_piece, weight_piece.T, preferred_element_type=jnp.float32)
        return running + rounded(product)

    start_sum = jnp.zeros((left_rows.shape[0], weight.shape[0]), jnp.float32)
    return lax.fori_loop(0, N_COL, add_block, start_sum)


def grouped(field):
    shaped = field.reshape(N_DP, STATES_DEV, N_ROW, PLANES, TILE_X, TILE_Y, field.shape[-1])
    shaped = jnp.transpose(shaped, (0, 2, 1, 3, 4, 5, 6))
    return shaped.reshape(N_DP * N_ROW, STATES_DEV * PLANES * TILE_X * TILE_Y, field.shape[-1])


def group_products(left_field, right_field):
    left_groups = grouped(left_field)
    right_groups = grouped(right_field)

    def add_group(running, pieces):
        product = jnp.dot(pieces[0].T, pieces[1], preferred_element_type=jnp.float32)
        return running + rounded(product), None

    start_sum = jnp.zeros((left_groups.shape[2], right_groups.shape[2]), jnp.float32)
    running, unused = lax.scan(add_group, start_sum, (left_groups, right_groups))
    return running


def reference(inputs, up_weight, down_weight, kernel, cotangent):
    full_width = inputs.shape[4]
    flat_inputs = inputs.reshape(-1, full_width)
    flat_cotangent = cotangent.reshape(-1, full_width)
    field_shape = inputs.shape[:4] + (EXPAND,)
    hidden = jnp.dot(flat_inputs, up_weight, preferred_element_type=jnp.float32).astype(jnp.bfloat16).reshape(field_shape)
    hidden_pad = pad_field(hidden)
    preact = stencil_sum(hidden_pad, kernel, 0, DEPTH, TILE_X, TILE_Y)
    activation = jax.nn.silu(preact).astype(jnp.bfloat16)
    flat_act = activation.reshape(-1, EXPAND)
    block_output = (inputs.astype(jnp.float32) + block_products(flat_act, down_weight).reshape(inputs.shape)).astype(jnp.bfloat16)
    act_grad = jnp.dot(flat_cotangent, down_weight, preferred_element_type=jnp.float32).reshape(field_shape)
    logistic = jax.nn.sigmoid(preact)
    preact_grad = (act_grad * logistic * (1.0 + preact * (1.0 - logistic))).astype(jnp.bfloat16)
    grad_pad = pad_field(preact_grad)
    hidden_grad = stencil_sum(grad_pad, kernel, 1, DEPTH, TILE_X, TILE_Y).astype(jnp.bfloat16)
    kernel_grad = kernel_terms(hidden_pad, preact_grad, DEPTH, TILE_X, TILE_Y)
    flat_grad_hidden = hidden_grad.reshape(-1, EXPAND)
    input_grad = (cotangent.astype(jnp.float32) + block_products(flat_grad_hidden, up_weight).reshape(inputs.shape)).astype(jnp.bfloat16)
    up_grad = group_products(inputs, hidden_grad).astype(jnp.bfloat16)
    down_grad = group_products(cotangent, activation).astype(jnp.bfloat16)
    return (block_output, input_grad, up_grad, down_grad, kernel_grad)
```

```python
import functools

import jax
import jax.numpy as jnp
from jax import lax
from jax.experimental import pallas as pl
from jax.experimental.pallas import tpu as pltpu
from jax.sharding import PartitionSpec as P

LANES = 128


def lane_block(index):
    return pl.ds(pl.multiple_of(index * LANES, LANES), LANES)


def clear_windows(win):
    halves, depth, tile_x, _, lanes = win.shape
    zeros = jnp.zeros((8, lanes), jnp.float32)
    for z in range(depth):
        for x in range(tile_x):
            win[0, z, x, 0:8] = zeros
            win[halves - 1, z, x, 16:24] = zeros


def fill_windows(win, field, cols):
    halves, depth, tile_x, _, _ = win.shape
    for z in range(depth):
        for x in range(tile_x):
            line = field[z, x, :, cols].astype(jnp.float32)
            for h in range(halves):
                for part in range(3):
                    first = 8 * (h + part - 1)
                    if 0 <= first < 8 * halves:
                        win[h, z, x, 8 * part : 8 * part + 8] = line[first : first + 8]


def pairs(source_z, source_x, planes, tile_x):
    for a in range(5):
        z = source_z - a
        if 0 <= z < planes:
            for b in range(5):
                x = source_x - b + 2
                if 0 <= x < tile_x:
                    yield a, b, z, x


def stencil_half(win, half, kernel, cols, mirror, planes, tile_x):
    accs = [[None] * tile_x for _ in range(planes)]
    for c in range(5):
        taps = {}
        for a in range(5):
            for b in range(5):
                t = 25 * a + 5 * b + c
                t = 124 - t if mirror else t
                taps[a, b] = jnp.broadcast_to(kernel[t : t + 1, cols], (8, LANES))
        for sz in range(planes + 4):
            for sx in range(tile_x):
                cells = win[half, sz, sx, 6 + c : 14 + c]
                for a, b, z, x in pairs(sz, sx, planes, tile_x):
                    term = taps[a, b] * cells
                    accs[z][x] = term if accs[z][x] is None else accs[z][x] + term
    return accs


def tap_sums(win, grad, cols, planes, tile_x, halves, store):
    for c in range(5):
        def one_half(half, sums):
            sums = list(sums)
            rows = pl.ds(pl.multiple_of(half * 8, 8), 8)
            grads = [[grad[z, x, rows, :] for x in range(tile_x)] for z in range(planes)]
            for sz in range(planes + 4):
                for sx in range(tile_x):
                    cells = win[half, sz, sx, 6 + c : 14 + c]
                    for a, b, z, x in pairs(sz, sx, planes, tile_x):
                        sums[5 * a + b] = sums[5 * a + b] + cells * grads[z][x]
            return tuple(sums)

        sums = lax.fori_loop(0, halves, one_half, (jnp.zeros((8, LANES), jnp.float32),) * 25)
        for ab in range(25):
            store(5 * ab + c, jnp.sum(sums[ab], axis=0, keepdims=True))


def forward_kernel(field, kernel, out, win):
    planes, tile_x = out.shape[:2]
    halves = win.shape[0]
    clear_windows(win)

    @pl.loop(0, out.shape[3] // LANES)
    def _(block):
        cols = lane_block(block)
        fill_windows(win, field, cols)

        @pl.loop(0, halves)
        def _(half):
            rows = pl.ds(pl.multiple_of(half * 8, 8), 8)
            accs = stencil_half(win, half, kernel, cols, False, planes, tile_x)
            for z in range(planes):
                for x in range(tile_x):
                    out[z, x, rows, cols] = accs[z][x]


def backward_kernel(field, kernel, out, win, tmp):
    planes, tile_x = out.shape[:2]
    halves = win.shape[0]
    clear_windows(win)

    @pl.loop(0, out.shape[3] // LANES)
    def _(block):
        cols = lane_block(block)
        fill_windows(win, field, cols)

        @pl.loop(0, halves)
        def _(half):
            rows = pl.ds(pl.multiple_of(half * 8, 8), 8)
            accs = stencil_half(win, half, kernel, cols, True, planes, tile_x)
            for z in range(planes):
                for x in range(tile_x):
                    tmp[z, x, rows, :] = accs[z][x]

        for z in range(planes):
            for x in range(tile_x):
                out[z, x, :, cols] = tmp[z, x].astype(out.dtype)


def taps_kernel(field, grad, out, win, tmp):
    planes, tile_x = grad.shape[:2]
    halves = win.shape[0]
    clear_windows(win)

    @pl.loop(0, out.shape[1] // LANES)
    def _(block):
        cols = lane_block(block)
        fill_windows(win, field, cols)
        for z in range(planes):
            for x in range(tile_x):
                tmp[z, x] = grad[z, x, :, cols].astype(jnp.float32)

        def store(t, row):
            out[t : t + 1, cols] = row

        tap_sums(win, tmp, cols, planes, tile_x, halves, store)


def call(body, out_shape, shape, scratch_tmp, args):
    planes, tile_x, tile_y, _ = shape
    scratch = [pltpu.VMEM((tile_y // 8, planes + 4, tile_x, 24, LANES), jnp.float32)]
    if scratch_tmp:
        scratch.append(pltpu.VMEM((planes, tile_x, tile_y, LANES), jnp.float32))
    return pl.pallas_call(
        body,
        out_shape=out_shape,
        in_specs=[pl.BlockSpec(memory_space=pltpu.VMEM)] * len(args),
        out_specs=pl.BlockSpec(memory_space=pltpu.VMEM),
        scratch_shapes=scratch,
        compiler_params=pltpu.CompilerParams(vmem_limit_bytes=24 << 20),
        cost_estimate=pl.CostEstimate(flops=10**10, bytes_accessed=3 * 10**6, transcendentals=0),
    )(*args)


def with_halo(shard, width):
    peers, length = (lax.axis_size("row"), shard.shape[0])
    up = [(i, (i + 1) % peers) for i in range(peers - 1)]
    down = [(j, i) for i, j in up]
    before = lax.ppermute(lax.slice_in_dim(shard, length - width, length, axis=0), "row", up)
    after = lax.ppermute(lax.slice_in_dim(shard, 0, width, axis=0), "row", down)
    return jnp.concatenate([before, shard, after], axis=0)


def column_sum(partial_value, field_shape):
    return lax.psum_scatter(
        partial_value.reshape(field_shape).astype(jnp.bfloat16),
        "col",
        scatter_dimension=4,
        tiled=True,
    ).astype(jnp.float32)


def spread_product(left_rows, right_rows):
    product = lax.dot_general(
        left_rows, right_rows, (((0,), (0,)), ((), ())), preferred_element_type=jnp.float32
    ).astype(jnp.bfloat16)
    return lax.psum_scatter(product, ("dp", "row"), scatter_dimension=0, tiled=True)


def on_device(inputs, up_weight, down_weight, kernel, cotangent):
    states, planes, tile_x, tile_y, _ = inputs.shape
    voxels = planes * tile_x * tile_y
    local_hidden = up_weight.shape[1]
    contract_last = (((1,), (1,)), ((), ()))
    input_rows = lax.all_gather(inputs, "col", axis=4, tiled=True)
    cotangent_rows = lax.all_gather(cotangent, "col", axis=4, tiled=True)
    full_width = input_rows.shape[4]
    field_shape = (states, planes, tile_x, tile_y, full_width)
    shape = (planes, tile_x, tile_y, local_hidden)
    flat_inputs = input_rows.reshape(voxels, full_width)
    hidden = jnp.dot(flat_inputs, up_weight, preferred_element_type=jnp.float32)
    hidden_ext = with_halo(hidden.astype(jnp.bfloat16).reshape(shape), 2)
    preact = call(forward_kernel, jax.ShapeDtypeStruct(shape, jnp.float32), shape, False, (hidden_ext, kernel))
    activation = jax.nn.silu(preact).astype(jnp.bfloat16)
    flat_act = activation.reshape(voxels, local_hidden)
    flat_cotangent = cotangent_rows.reshape(voxels, full_width)
    down_grad = spread_product(flat_cotangent, flat_act)
    mixed_share = column_sum(
        lax.dot_general(flat_act, down_weight, contract_last, preferred_element_type=jnp.float32),
        field_shape,
    )
    block_output = (inputs.astype(jnp.float32) + mixed_share).astype(jnp.bfloat16)
    act_grad = jnp.dot(flat_cotangent, down_weight, preferred_element_type=jnp.float32).reshape(shape)
    logistic = jax.nn.sigmoid(preact)
    preact_grad = (act_grad * logistic * (1.0 + preact * (1.0 - logistic))).astype(jnp.bfloat16)
    grad_ext = with_halo(preact_grad, 2)
    kernel_grad = call(
        taps_kernel, jax.ShapeDtypeStruct(kernel.shape, jnp.float32), shape, True, (hidden_ext, preact_grad)
    )
    kernel_grad = lax.psum(kernel_grad.astype(jnp.bfloat16), ("dp", "row")).astype(jnp.float32)
    hidden_grad = call(
        backward_kernel, jax.ShapeDtypeStruct(shape, jnp.bfloat16), shape, True, (grad_ext, kernel)
    )
    flat_grad_hidden = hidden_grad.reshape(voxels, local_hidden)
    up_grad = spread_product(flat_inputs, flat_grad_hidden)
    input_share = column_sum(
        lax.dot_general(
            flat_grad_hidden, up_weight, contract_last, preferred_element_type=jnp.float32
        ),
        field_shape,
    )
    input_grad = (cotangent.astype(jnp.float32) + input_share).astype(jnp.bfloat16)
    return (block_output, input_grad, up_grad, down_grad, kernel_grad)


def solution(mesh):
    placed = (
        P("dp", "row", None, None, "col"),
        P(None, "col"),
        P(None, "col"),
        P(None, "col"),
        P("dp", "row", None, None, "col"),
    )
    return jax.shard_map(
        on_device,
        mesh=mesh,
        in_specs=placed,
        out_specs=(
            P("dp", "row", None, None, "col"),
            P("dp", "row", None, None, "col"),
            P(("dp", "row"), "col"),
            P(("dp", "row"), "col"),
            P(None, "col"),
        ),
        check_vma=False,
    )
```

```python
import functools

import jax
import jax.numpy as jnp
from jax import lax
from jax.experimental import pallas as pl
from jax.experimental.pallas import tpu as pltpu
from jax.sharding import PartitionSpec as P

LANES = 128
HALO = 2


def aligned(index, size):
    return pl.ds(pl.multiple_of(index * size, size), size)


def clear_windows(win):
    halves, depth, tile_x, _, lanes = win.shape
    zeros = jnp.zeros((8, lanes), jnp.float32)
    for z in range(depth):
        for x in range(tile_x):
            win[0, z, x, 0:8] = zeros
            win[halves - 1, z, x, 16:24] = zeros


def fill_windows(win, field, cols):
    halves, depth, tile_x, _, _ = win.shape
    tile_y = 8 * halves
    for z in range(depth):
        for x in range(tile_x):
            first_row = (z * tile_x + x) * tile_y
            line = field[first_row : first_row + tile_y, cols].astype(jnp.float32)
            for h in range(halves):
                for part in range(3):
                    first = 8 * (h + part - 1)
                    if 0 <= first < tile_y:
                        win[h, z, x, 8 * part : 8 * part + 8] = line[first : first + 8]


def pairs(source_z, source_x, planes, tile_x):
    for a in range(5):
        z = source_z - a
        if 0 <= z < planes:
            for b in range(5):
                x = source_x - b + 2
                if 0 <= x < tile_x:
                    yield a, b, z, x


def stencil_half(win, half, kernel, cols, mirror, planes, tile_x):
    accs = [[None] * tile_x for _ in range(planes)]
    for c in range(5):
        taps = {}
        for a in range(5):
            for b in range(5):
                t = 25 * a + 5 * b + c
                t = 124 - t if mirror else t
                taps[a, b] = jnp.broadcast_to(kernel[t : t + 1, cols], (8, LANES))
        for sz in range(planes + 2 * HALO):
            for sx in range(tile_x):
                cells = win[half, sz, sx, 6 + c : 14 + c]
                for a, b, z, x in pairs(sz, sx, planes, tile_x):
                    term = taps[a, b] * cells
                    accs[z][x] = term if accs[z][x] is None else accs[z][x] + term
    return accs


def stencil(win, field, kernel, mirror, planes, tile_x, wide, finish):
    halves = win.shape[0]
    tile_y = 8 * halves

    @pl.loop(0, kernel.shape[1] // LANES)
    def _(block):
        cols = aligned(block, LANES)
        fill_windows(win, field, cols)

        @pl.loop(0, halves)
        def _(half):
            accs = stencil_half(win, half, kernel, cols, mirror, planes, tile_x)
            for z in range(planes):
                for x in range(tile_x):
                    first = (z * tile_x + x) * tile_y + half * 8
                    wide[pl.ds(pl.multiple_of(first, 8), 8), cols] = accs[z][x]

        for line in range(planes * tile_x):
            rows = slice(line * tile_y, (line + 1) * tile_y)
            finish(rows, cols, wide[rows, cols])


def tap_sums(win, tmp, field, grad, out, planes, tile_x):
    halves = win.shape[0]
    tile_y = 8 * halves
    first_row = HALO * tile_x * tile_y

    @pl.loop(0, out.shape[1] // LANES)
    def _(block):
        cols = aligned(block, LANES)
        fill_windows(win, field, cols)
        for line in range(planes * tile_x):
            rows = slice(first_row + line * tile_y, first_row + (line + 1) * tile_y)
            tmp[line] = grad[rows, cols].astype(jnp.float32)
        for c in range(5):
            def one_half(half, sums):
                sums = list(sums)
                rows = aligned(half, 8)
                grads = [tmp[line, rows, :] for line in range(planes * tile_x)]
                for sz in range(planes + 2 * HALO):
                    for sx in range(tile_x):
                        cells = win[half, sz, sx, 6 + c : 14 + c]
                        for a, b, z, x in pairs(sz, sx, planes, tile_x):
                            sums[5 * a + b] = sums[5 * a + b] + cells * grads[z * tile_x + x]
                return tuple(sums)

            sums = lax.fori_loop(0, halves, one_half, (jnp.zeros((8, LANES), jnp.float32),) * 25)
            for ab in range(25):
                t = 5 * ab + c
                out[t : t + 1, cols] = jnp.sum(sums[ab], axis=0, keepdims=True)


def block_kernel(
    sizes, inputs, cotangent, up_weight, down_weight, kernel,
    block_output, input_grad, up_grad, down_grad, kernel_grad,
    xg, cg, upw, dnw, hid, grd, wide, act, hgr, win, tmp, sent, got, turned,
    first_out, first_in, second_out, second_in, taps, taps_out, taps_in, share_out, share_in, half_out, half_in,
    load_sem, ag_s, ag_r, halo_s, halo_r, rs_s, rs_r, pair_s, pair_r, row_s, row_r, kg_s, kg_r,
):
    planes, tile_x, tile_y, n_dp, n_row, n_col = sizes
    dp, row, col = lax.axis_index("dp"), lax.axis_index("row"), lax.axis_index("col")
    partner = {"dp": 1 - dp}
    voxels, local = inputs.shape
    channels = kernel.shape[1]
    plane = tile_x * tile_y
    own = slice(HALO * plane, HALO * plane + voxels)
    tile = min(256, channels)
    wtile = min(256, local)
    n_half = n_col // 2
    share = first_out.shape[1] * local // n_row
    bf16, f32 = jnp.bfloat16, jnp.float32
    mine = aligned(col, local)

    loads = [
        pltpu.make_async_copy(source, target, load_sem.at[i])
        for i, (source, target) in enumerate(
            ((inputs, xg.at[:, mine]), (up_weight, upw), (cotangent, cg.at[:, mine]), (down_weight, dnw))
        )
    ]
    for load in loads:
        load.start()

    barrier = pltpu.get_barrier_semaphore()

    @pl.loop(1, n_col)
    def _(k):
        pl.semaphore_signal(barrier, inc=1, device_id={"col": lax.rem(col + k, n_col)})

    @pl.loop(1, n_row)
    def _(k):
        pl.semaphore_signal(barrier, inc=1, device_id={"row": lax.rem(row + k, n_row)})

    pl.semaphore_signal(barrier, inc=1, device_id=partner)
    pl.semaphore_wait(barrier, n_col + n_row - 1)

    def remote(source, target, send, receive, device):
        return pltpu.make_async_remote_copy(
            src_ref=source, dst_ref=target, send_sem=send, recv_sem=receive,
            device_id=device, device_id_type=pl.DeviceIdType.MESH,
        )

    def gather(i, k):
        source, target = ((inputs, xg), (cotangent, cg))[i]
        return remote(
            source, target.at[:, mine], ag_s.at[i, k], ag_r.at[i, k], {"col": lax.rem(col + k, n_col)}
        )

    def each(count, action, first=1):
        @pl.loop(first, count)
        def _(k):
            action(k)

    each(n_col, lambda k: gather(0, k).start())
    each(n_col, lambda k: gather(0, k).wait_send())
    each(n_col, lambda k: gather(1, k).start())
    clear_windows(win)
    each(n_col, lambda k: gather(0, k).wait_recv())
    loads[0].wait()
    loads[1].wait()

    @pl.loop(0, channels // tile)
    def _(n):
        cols = aligned(n, tile)
        hid[own, cols] = jnp.dot(xg[...], upw[:, cols], preferred_element_type=f32).astype(bf16)

    def halo(i, field, side):
        if side:
            source, target, peer = field.at[HALO * plane : 2 * HALO * plane], voxels + HALO * plane, row - 1
        else:
            source, target, peer = field.at[voxels : voxels + HALO * plane], 0, row + 1
        return remote(
            source, field.at[target : target + HALO * plane], halo_s.at[i, side], halo_r.at[i, side], {"row": peer}
        )

    def halo_start(i, field):
        @pl.when(row < n_row - 1)
        def _():
            halo(i, field, 0).start()

        @pl.when(row > 0)
        def _():
            halo(i, field, 1).start()

        @pl.when(row == 0)
        def _():
            field[0 : HALO * plane] = jnp.zeros((HALO * plane, channels), bf16)

        @pl.when(row == n_row - 1)
        def _():
            field[voxels + HALO * plane :] = jnp.zeros((HALO * plane, channels), bf16)

    def halo_wait(i, field):
        @pl.when(row > 0)
        def _():
            halo(i, field, 0).wait_recv()
            halo(i, field, 1).wait_send()

        @pl.when(row < n_row - 1)
        def _():
            halo(i, field, 1).wait_recv()
            halo(i, field, 0).wait_send()

    halo_start(0, hid)
    halo_wait(0, hid)

    def activate(rows, cols, preact):
        act[rows, cols] = (preact * jax.nn.sigmoid(preact)).astype(bf16)

    stencil(win, hid, kernel, False, planes, tile_x, wide, activate)

    loads[2].wait()
    loads[3].wait()
    each(n_col, lambda k: gather(1, k).wait_recv())

    @pl.loop(0, channels // tile)
    def _(n):
        cols = aligned(n, tile)
        act_grad = jnp.dot(cg[...], dnw[:, cols], preferred_element_type=f32)
        preact = wide[:, cols]
        logistic = jax.nn.sigmoid(preact)
        grd[own, cols] = (act_grad * logistic * (1.0 + preact * (1.0 - logistic))).astype(bf16)

    halo_start(1, grd)

    def pair(i, j):
        return remote(first_out.at[i, j], first_in.at[i, j], pair_s.at[i, j], pair_r.at[i, j], partner)

    def turn(left, chunk):
        turned[...] = left[:, aligned(chunk, local)].T

    def grad_for_partner(i, left, right):
        @pl.loop(0, n_half)
        def _(j):
            turn(left, (1 - dp) * n_half + j)

            @pl.loop(0, channels // tile)
            def _(n):
                cols = aligned(n, tile)
                first_out[i, j, :, cols] = jnp.dot(
                    turned[...], right[:, cols], preferred_element_type=f32
                ).astype(bf16)

            pair(i, j).start()

    def row_copy(i, k):
        peer = lax.rem(row + k, n_row)
        return remote(
            second_out.at[i, aligned(peer, share)], second_in.at[i, k], row_s.at[i, k], row_r.at[i, k], {"row": peer}
        )

    def grad_own(i, left, right):
        @pl.loop(0, n_half)
        def _(j):
            turn(left, dp * n_half + j)
            pair(i, j).wait_recv()

            @pl.loop(0, channels // tile)
            def _(n):
                cols = aligned(n, tile)
                product = jnp.dot(turned[...], right[:, cols], preferred_element_type=f32).astype(bf16)
                both = product.astype(f32) + first_in[i, j, :, cols].astype(f32)
                second_out[i, aligned(j, local), cols] = both.astype(bf16)

        each(n_row, lambda k: row_copy(i, k).start())

    def grad_finish(i, out):
        each(n_row, lambda k: row_copy(i, k).wait_recv())

        @pl.loop(0, channels // tile)
        def _(n):
            cols = aligned(n, tile)
            total = second_out[i, aligned(row, share), cols].astype(f32)
            for k in range(1, n_row):
                total = total + second_in[i, k, :, cols].astype(f32)
            out[:, cols] = total.astype(bf16)

        each(n_row, lambda k: row_copy(i, k).wait_send())
        each(n_half, lambda j: pair(i, j).wait_send(), 0)

    def column_copy(i, k):
        return remote(sent.at[i, k], got.at[i, k], rs_s.at[i, k], rs_r.at[i, k], {"col": lax.rem(col + k, n_col)})

    def column_partials(i, left, weight):
        def one(k):
            first = lax.rem(col + k, n_col) * local

            @pl.loop(0, local // wtile)
            def _(n):
                rows = pl.ds(pl.multiple_of(first + n * wtile, wtile), wtile)
                product = lax.dot_general(
                    left[...], weight[rows, :], (((1,), (1,)), ((), ())), preferred_element_type=f32
                )
                sent[i, k, :, aligned(n, wtile)] = product.astype(bf16)

        @pl.loop(1, n_col)
        def _(k):
            one(k)
            column_copy(i, k).start()

        one(0)

    def column_finish(i, residual, out):
        each(n_col, lambda k: column_copy(i, k).wait_recv())
        total = sent[i, 0].astype(f32)
        for k in range(1, n_col):
            total = total + got[i, k].astype(f32)
        out[...] = (residual[:, mine].astype(f32) + total).astype(bf16)
        each(n_col, lambda k: column_copy(i, k).wait_send())

    column_partials(0, act, dnw)
    grad_for_partner(0, cg, act)

    tap_sums(win, tmp, hid, grd, taps, planes, tile_x)
    taps_out[0 : kernel.shape[0]] = taps[0 : kernel.shape[0]].astype(bf16)
    taps_out[kernel.shape[0] :] = jnp.zeros((taps_out.shape[0] - kernel.shape[0], channels), bf16)
    whole_taps = remote(taps_out, taps_in, kg_s.at[0], kg_r.at[0], partner)
    whole_taps.start()
    halo_wait(1, grd)
    grad_own(0, cg, act)

    def keep(rows, cols, total):
        hgr[rows, cols] = total.astype(bf16)

    stencil(win, grd, kernel, True, planes, tile_x, wide, keep)
    grad_for_partner(1, xg, hgr)
    column_partials(1, hgr, upw)
    grad_own(1, xg, hgr)

    whole_taps.wait_recv()
    some = aligned(dp, channels // 2)
    share_out[...] = (taps_out[:, some].astype(f32) + taps_in[:, some].astype(f32)).astype(bf16)

    def taps_copy(k):
        return remote(share_out, share_in.at[k], kg_s.at[k], kg_r.at[k], {"row": lax.rem(row + k, n_row)})

    each(n_row, lambda k: taps_copy(k).start())
    column_finish(0, xg, block_output)
    grad_finish(0, down_grad)
    each(n_row, lambda k: taps_copy(k).wait_recv())
    total = share_out[...].astype(f32)
    for k in range(1, n_row):
        total = total + share_in[k].astype(f32)
    half_out[...] = total
    halves = remote(half_out, half_in, kg_s.at[n_row], kg_r.at[n_row], partner)
    halves.start()
    kernel_grad[:, some] = half_out[0 : kernel.shape[0]]
    column_finish(1, cg, input_grad)
    halves.wait_recv()
    kernel_grad[:, aligned(1 - dp, channels // 2)] = half_in[0 : kernel.shape[0]]
    grad_finish(1, up_grad)
    each(n_col, lambda k: gather(1, k).wait_send())
    whole_taps.wait_send()
    each(n_row, lambda k: taps_copy(k).wait_send())
    halves.wait_send()


def on_device(inputs, up_weight, down_weight, kernel, cotangent):
    _, planes, tile_x, tile_y, local = inputs.shape
    n_dp, n_row, n_col = (lax.axis_size(name) for name in ("dp", "row", "col"))
    voxels = planes * tile_x * tile_y
    extended = voxels + 2 * HALO * tile_x * tile_y
    width, channels = up_weight.shape
    share = width // (n_dp * n_row)
    bf16, f32 = jnp.bfloat16, jnp.float32
    dma = pltpu.SemaphoreType.DMA
    taps = kernel.shape[0]
    tap_rows = -(-taps // 16) * 16
    vmem, anywhere = pl.BlockSpec(memory_space=pltpu.VMEM), pl.BlockSpec(memory_space=pl.ANY)
    outs = pl.pallas_call(
        functools.partial(block_kernel, (planes, tile_x, tile_y, n_dp, n_row, n_col)),
        out_shape=(
            jax.ShapeDtypeStruct((voxels, local), bf16),
            jax.ShapeDtypeStruct((voxels, local), bf16),
            jax.ShapeDtypeStruct((share, channels), bf16),
            jax.ShapeDtypeStruct((share, channels), bf16),
            jax.ShapeDtypeStruct((taps, channels), f32),
        ),
        in_specs=[anywhere] * 4 + [vmem],
        out_specs=(vmem,) * 5,
        scratch_shapes=[
            pltpu.VMEM((voxels, width), bf16),
            pltpu.VMEM((voxels, width), bf16),
            pltpu.VMEM((width, channels), bf16),
            pltpu.VMEM((width, channels), bf16),
            pltpu.VMEM((extended, channels), bf16),
            pltpu.VMEM((extended, channels), bf16),
            pltpu.VMEM((voxels, channels), f32),
            pltpu.VMEM((voxels, channels), bf16),
            pltpu.VMEM((voxels, channels), bf16),
            pltpu.VMEM((tile_y // 8, planes + 2 * HALO, tile_x, 24, LANES), f32),
            pltpu.VMEM((planes * tile_x, tile_y, LANES), f32),
            pltpu.VMEM((2, n_col, voxels, local), bf16),
            pltpu.VMEM((2, n_col, voxels, local), bf16),
            pltpu.VMEM((local, voxels), bf16),
            pltpu.VMEM((2, n_col // 2, local, channels), bf16),
            pltpu.VMEM((2, n_col // 2, local, channels), bf16),
            pltpu.VMEM((2, width // 2, channels), bf16),
            pltpu.VMEM((2, n_row, share, channels), bf16),
            pltpu.VMEM((tap_rows, channels), f32),
            pltpu.VMEM((tap_rows, channels), bf16),
            pltpu.VMEM((tap_rows, channels), bf16),
            pltpu.VMEM((tap_rows, channels // 2), bf16),
            pltpu.VMEM((n_row, tap_rows, channels // 2), bf16),
            pltpu.VMEM((tap_rows, channels // 2), f32),
            pltpu.VMEM((tap_rows, channels // 2), f32),
            dma((4,)),
            dma((2, n_col)), dma((2, n_col)),
            dma((2, 2)), dma((2, 2)),
            dma((2, n_col)), dma((2, n_col)),
            dma((2, n_col // 2)), dma((2, n_col // 2)),
            dma((2, n_row)), dma((2, n_row)),
            dma((n_row + 1,)), dma((n_row + 1,)),
        ],
        compiler_params=pltpu.CompilerParams(
            collective_id=0, has_side_effects=True, vmem_limit_bytes=56 << 20
        ),
    )(inputs.reshape(voxels, local), cotangent.reshape(voxels, local), up_weight, down_weight, kernel)
    return (outs[0].reshape(inputs.shape), outs[1].reshape(inputs.shape)) + tuple(outs[2:])


def solution(mesh):
    placed = (
        P("dp", "row", None, None, "col"),
        P(None, "col"),
        P(None, "col"),
        P(None, "col"),
        P("dp", "row", None, None, "col"),
    )
    return jax.shard_map(
        on_device,
        mesh=mesh,
        in_specs=placed,
        out_specs=(
            P("dp", "row", None, None, "col"),
            P("dp", "row", None, None, "col"),
            P(("dp", "row"), "col"),
            P(("dp", "row"), "col"),
            P(None, "col"),
        ),
        check_vma=False,
    )
```

```python
import functools

import jax
import jax.numpy as jnp
from jax import lax
from jax.experimental import pallas as pl
from jax.experimental.pallas import tpu as pltpu
from jax.sharding import PartitionSpec as P

LANES = 128
HALO = 2


def aligned(index, size):
    return pl.ds(pl.multiple_of(index * size, size), size)


def clear_windows(win):
    halves, depth, tile_x, _, lanes = win.shape
    zeros = jnp.zeros((8, lanes), jnp.float32)
    for z in range(depth):
        for x in range(tile_x):
            win[0, z, x, 0:8] = zeros
            win[halves - 1, z, x, 16:24] = zeros


def fill_windows(win, field, cols):
    halves, depth, tile_x, _, _ = win.shape
    tile_y = 8 * halves
    for z in range(depth):
        for x in range(tile_x):
            first_row = (z * tile_x + x) * tile_y
            line = field[first_row : first_row + tile_y, cols].astype(jnp.float32)
            for h in range(halves):
                for part in range(3):
                    first = 8 * (h + part - 1)
                    if 0 <= first < tile_y:
                        win[h, z, x, 8 * part : 8 * part + 8] = line[first : first + 8]


def pairs(source_z, source_x, planes, tile_x):
    for a in range(5):
        z = source_z - a
        if 0 <= z < planes:
            for b in range(5):
                x = source_x - b + 2
                if 0 <= x < tile_x:
                    yield a, b, z, x


def stencil_half(win, half, kernel, cols, mirror, planes, tile_x):
    accs = [[None] * tile_x for _ in range(planes)]
    for c in range(5):
        taps = {}
        for a in range(5):
            for b in range(5):
                t = 25 * a + 5 * b + c
                t = 124 - t if mirror else t
                taps[a, b] = jnp.broadcast_to(kernel[t : t + 1, cols], (8, LANES))
        for sz in range(planes + 2 * HALO):
            for sx in range(tile_x):
                cells = win[half, sz, sx, 6 + c : 14 + c]
                for a, b, z, x in pairs(sz, sx, planes, tile_x):
                    term = taps[a, b] * cells
                    accs[z][x] = term if accs[z][x] is None else accs[z][x] + term
    return accs


def stencil(win, field, kernel, mirror, planes, tile_x, wide, finish, midway=None):
    halves = win.shape[0]
    tile_y = 8 * halves

    @pl.loop(0, kernel.shape[1] // LANES)
    def _(block):
        cols = aligned(block, LANES)
        fill_windows(win, field, cols)
        if midway is not None:
            pl.when(block == kernel.shape[1] // LANES // 2)(midway)

        @pl.loop(0, halves)
        def _(half):
            accs = stencil_half(win, half, kernel, cols, mirror, planes, tile_x)
            for z in range(planes):
                for x in range(tile_x):
                    first = (z * tile_x + x) * tile_y + half * 8
                    wide[pl.ds(pl.multiple_of(first, 8), 8), cols] = accs[z][x]

        for line in range(planes * tile_x):
            rows = slice(line * tile_y, (line + 1) * tile_y)
            finish(rows, cols, wide[rows, cols])


def tap_sums(win, tmp, field, grad, out, planes, tile_x):
    halves = win.shape[0]
    tile_y = 8 * halves
    first_row = HALO * tile_x * tile_y

    @pl.loop(0, out.shape[1] // LANES)
    def _(block):
        cols = aligned(block, LANES)
        fill_windows(win, field, cols)
        for line in range(planes * tile_x):
            rows = slice(first_row + line * tile_y, first_row + (line + 1) * tile_y)
            tmp[line] = grad[rows, cols].astype(jnp.float32)
        for c in range(5):
            def one_half(half, sums):
                sums = list(sums)
                rows = aligned(half, 8)
                grads = [tmp[line, rows, :] for line in range(planes * tile_x)]
                for sz in range(planes + 2 * HALO):
                    for sx in range(tile_x):
                        cells = win[half, sz, sx, 6 + c : 14 + c]
                        for a, b, z, x in pairs(sz, sx, planes, tile_x):
                            sums[5 * a + b] = sums[5 * a + b] + cells * grads[z * tile_x + x]
                return tuple(sums)

            sums = lax.fori_loop(0, halves, one_half, (jnp.zeros((8, LANES), jnp.float32),) * 25)
            for ab in range(25):
                t = 5 * ab + c
                out[t : t + 1, cols] = jnp.sum(sums[ab], axis=0, keepdims=True)


def block_kernel(
    sizes, inputs, cotangent, up_weight, down_weight, stencil_weights,
    block_output, input_grad, up_grad, down_grad, kernel_grad,
    kernel, xg, cg, upw, dnw, hid, grd, wide, act, hgr, win, tmp, sent, got, turned,
    first_out, first_in, second_out, second_in, taps, taps_out, taps_in, share_out, share_in, half_out, half_in,
    load_sem, ag_s, ag_r, halo_s, halo_r, rs_s, rs_r, pair_s, pair_r, row_s, row_r, kg_s, kg_r,
):
    planes, tile_x, tile_y, n_dp, n_row, n_col = sizes
    dp, row, col = lax.axis_index("dp"), lax.axis_index("row"), lax.axis_index("col")
    partner = {"dp": 1 - dp}
    voxels, local = inputs.shape
    channels = kernel.shape[1]
    plane = tile_x * tile_y
    own = slice(HALO * plane, HALO * plane + voxels)
    tile = min(256, channels)
    wtile = min(256, local)
    n_half = n_col // 2
    share = first_out.shape[1] * local // n_row
    bf16, f32 = jnp.bfloat16, jnp.float32
    mine = aligned(col, local)

    loads = [
        pltpu.make_async_copy(source, target, load_sem.at[i])
        for i, (source, target) in enumerate(
            ((inputs, xg.at[:, mine]), (up_weight, upw), (stencil_weights, kernel), (cotangent, cg.at[:, mine]), (down_weight, dnw))
        )
    ]
    for load in loads:
        load.start()

    barrier = pltpu.get_barrier_semaphore()

    @pl.loop(1, n_col)
    def _(k):
        pl.semaphore_signal(barrier, inc=1, device_id={"col": lax.rem(col + k, n_col)})

    @pl.loop(1, n_row)
    def _(k):
        pl.semaphore_signal(barrier, inc=1, device_id={"row": lax.rem(row + k, n_row)})

    pl.semaphore_signal(barrier, inc=1, device_id=partner)
    pl.semaphore_wait(barrier, n_col + n_row - 1)

    def remote(source, target, send, receive, device):
        return pltpu.make_async_remote_copy(
            src_ref=source, dst_ref=target, send_sem=send, recv_sem=receive,
            device_id=device, device_id_type=pl.DeviceIdType.MESH,
        )

    def hop(i, side, step):
        gathered = (xg, cg)[i]
        source = (inputs, cotangent)[i] if step == 0 else gathered.at[:, aligned(col - side * step, local)]
        return remote(
            source, gathered.at[:, aligned(col - side * step, local)],
            ag_s.at[i, (side + 1) // 2, step], ag_r.at[i, (side + 1) // 2, step], {"col": col + side},
        )

    def inside(index):
        return jnp.logical_and(index >= 0, index < n_col)

    def hop_start(i, step):
        for side in (1, -1):
            pl.when(jnp.logical_and(inside(col + side), inside(col - side * step)))(hop(i, side, step).start)

    def hop_received(i, step):
        for side in (1, -1):
            pl.when(inside(col - side * (step + 1)))(hop(i, side, step).wait_recv)

    def hop_sent(i, step):
        for side in (1, -1):
            pl.when(jnp.logical_and(inside(col + side), inside(col - side * step)))(hop(i, side, step).wait_send)

    def advance(i, step):
        if step < n_col - 1:
            hop_received(i, step - 1)
            hop_start(i, step)

    def each(count, action, first=1):
        @pl.loop(first, count)
        def _(k):
            action(k)

    hop_start(0, 0)
    clear_windows(win)
    for step in range(1, n_col - 1):
        advance(0, step)
    hop_start(1, 0)
    hop_received(0, n_col - 2)
    loads[0].wait()
    loads[1].wait()

    @pl.loop(0, channels // tile)
    def _(n):
        cols = aligned(n, tile)
        hid[own, cols] = jnp.dot(xg[...], upw[:, cols], preferred_element_type=f32).astype(bf16)

    def turn(i, left):
        @pl.loop(0, n_col)
        def _(chunk):
            turned[i, aligned(chunk, local)] = left[:, aligned(chunk, local)].T

    def halo(i, field, side):
        if side:
            source, target, peer = field.at[HALO * plane : 2 * HALO * plane], voxels + HALO * plane, row - 1
        else:
            source, target, peer = field.at[voxels : voxels + HALO * plane], 0, row + 1
        return remote(
            source, field.at[target : target + HALO * plane], halo_s.at[i, side], halo_r.at[i, side], {"row": peer}
        )

    def halo_start(i, field):
        @pl.when(row < n_row - 1)
        def _():
            halo(i, field, 0).start()

        @pl.when(row > 0)
        def _():
            halo(i, field, 1).start()

        @pl.when(row == 0)
        def _():
            field[0 : HALO * plane] = jnp.zeros((HALO * plane, channels), bf16)

        @pl.when(row == n_row - 1)
        def _():
            field[voxels + HALO * plane :] = jnp.zeros((HALO * plane, channels), bf16)

    def halo_wait(i, field):
        @pl.when(row > 0)
        def _():
            halo(i, field, 0).wait_recv()
            halo(i, field, 1).wait_send()

        @pl.when(row < n_row - 1)
        def _():
            halo(i, field, 1).wait_recv()
            halo(i, field, 0).wait_send()

    halo_start(0, hid)
    advance(1, 1)
    turn(0, xg)
    loads[2].wait()
    halo_wait(0, hid)

    def activate(rows, cols, preact):
        act[rows, cols] = (preact * jax.nn.sigmoid(preact)).astype(bf16)

    stencil(win, hid, kernel, False, planes, tile_x, wide, activate, lambda: advance(1, 2))

    loads[3].wait()
    loads[4].wait()
    for step in range(3, n_col - 1):
        advance(1, step)
    hop_received(1, n_col - 2)

    @pl.loop(0, channels // tile)
    def _(n):
        cols = aligned(n, tile)
        act_grad = jnp.dot(cg[...], dnw[:, cols], preferred_element_type=f32)
        preact = wide[:, cols]
        logistic = jax.nn.sigmoid(preact)
        grd[own, cols] = (act_grad * logistic * (1.0 + preact * (1.0 - logistic))).astype(bf16)

    halo_start(1, grd)

    def pair(i, j):
        return remote(first_out.at[i, j], first_in.at[i, j], pair_s.at[i, j], pair_r.at[i, j], partner)

    def grad_for_partner(i, right):
        @pl.loop(0, n_half)
        def _(j):
            chunk = aligned((1 - dp) * n_half + j, local)

            @pl.loop(0, channels // tile)
            def _(n):
                cols = aligned(n, tile)
                first_out[i, j, :, cols] = jnp.dot(
                    turned[1 - i, chunk], right[:, cols], preferred_element_type=f32
                ).astype(bf16)

            pair(i, j).start()

    def row_copy(i, k):
        peer = lax.rem(row + k, n_row)
        return remote(
            second_out.at[i, aligned(peer, share)], second_in.at[i, k], row_s.at[i, k], row_r.at[i, k], {"row": peer}
        )

    def grad_own(i, right):
        @pl.loop(0, n_half)
        def _(j):
            chunk = aligned(dp * n_half + j, local)
            pair(i, j).wait_recv()

            @pl.loop(0, channels // tile)
            def _(n):
                cols = aligned(n, tile)
                product = jnp.dot(turned[1 - i, chunk], right[:, cols], preferred_element_type=f32).astype(bf16)
                both = product.astype(f32) + first_in[i, j, :, cols].astype(f32)
                second_out[i, aligned(j, local), cols] = both.astype(bf16)

            for part in range(local // share):
                peer = j * (local // share) + part
                k = lax.rem(peer - row + n_row, n_row)
                pl.when(peer != row)(lambda: row_copy(i, k).start())

    def grad_finish(i, out):
        each(n_row, lambda k: row_copy(i, k).wait_recv())

        @pl.loop(0, channels // tile)
        def _(n):
            cols = aligned(n, tile)
            total = second_out[i, aligned(row, share), cols].astype(f32)
            for k in range(1, n_row):
                total = total + second_in[i, k, :, cols].astype(f32)
            out[:, cols] = total.astype(bf16)

        each(n_row, lambda k: row_copy(i, k).wait_send())
        each(n_half, lambda j: pair(i, j).wait_send(), 0)

    def column_copy(i, k):
        return remote(sent.at[i, k], got.at[i, k], rs_s.at[i, k], rs_r.at[i, k], {"col": lax.rem(col + k, n_col)})

    def column_partials(i, left, weight):
        def one(k):
            first = lax.rem(col + k, n_col) * local

            @pl.loop(0, local // wtile)
            def _(n):
                rows = pl.ds(pl.multiple_of(first + n * wtile, wtile), wtile)
                product = lax.dot_general(
                    left[...], weight[rows, :], (((1,), (1,)), ((), ())), preferred_element_type=f32
                )
                sent[i, k, :, aligned(n, wtile)] = product.astype(bf16)

        @pl.loop(1, n_col)
        def _(k):
            one(k)
            column_copy(i, k).start()

        one(0)

    def column_finish(i, residual, out):
        each(n_col, lambda k: column_copy(i, k).wait_recv())
        total = sent[i, 0].astype(f32)
        for k in range(1, n_col):
            total = total + got[i, k].astype(f32)
        out[...] = (residual[:, mine].astype(f32) + total).astype(bf16)
        each(n_col, lambda k: column_copy(i, k).wait_send())

    turn(1, cg)
    grad_for_partner(0, act)
    column_partials(0, act, dnw)
    grad_own(0, act)
    halo_wait(1, grd)

    def keep(rows, cols, total):
        hgr[rows, cols] = total.astype(bf16)

    stencil(win, grd, kernel, True, planes, tile_x, wide, keep)
    grad_for_partner(1, hgr)
    column_partials(1, hgr, upw)
    grad_own(1, hgr)
    tap_sums(win, tmp, hid, grd, taps, planes, tile_x)
    taps_out[0 : kernel.shape[0]] = taps[0 : kernel.shape[0]].astype(bf16)
    taps_out[kernel.shape[0] :] = jnp.zeros((taps_out.shape[0] - kernel.shape[0], channels), bf16)
    whole_taps = remote(taps_out, taps_in, kg_s.at[0], kg_r.at[0], partner)
    whole_taps.start()
    column_finish(0, xg, block_output)
    whole_taps.wait_recv()
    some = aligned(dp, channels // 2)
    share_out[...] = (taps_out[:, some].astype(f32) + taps_in[:, some].astype(f32)).astype(bf16)

    def taps_copy(k):
        return remote(share_out, share_in.at[k], kg_s.at[k], kg_r.at[k], {"row": lax.rem(row + k, n_row)})

    each(n_row, lambda k: taps_copy(k).start())
    grad_finish(0, down_grad)
    column_finish(1, cg, input_grad)
    each(n_row, lambda k: taps_copy(k).wait_recv())
    total = share_out[...].astype(f32)
    for k in range(1, n_row):
        total = total + share_in[k].astype(f32)
    half_out[...] = total
    halves = remote(half_out, half_in, kg_s.at[n_row], kg_r.at[n_row], partner)
    halves.start()
    kernel_grad[:, some] = half_out[0 : kernel.shape[0]]
    grad_finish(1, up_grad)
    halves.wait_recv()
    kernel_grad[:, aligned(1 - dp, channels // 2)] = half_in[0 : kernel.shape[0]]
    for i in range(2):
        for step in range(n_col - 1):
            hop_sent(i, step)
    whole_taps.wait_send()
    each(n_row, lambda k: taps_copy(k).wait_send())
    halves.wait_send()


def hand_on(*refs):
    done = refs[10]
    copies = [pltpu.make_async_copy(refs[i], refs[5 + i], done.at[i]) for i in range(5)]
    for copy in copies:
        copy.start()
    for copy in copies:
        copy.wait()


def on_device(inputs, up_weight, down_weight, kernel, cotangent):
    _, planes, tile_x, tile_y, local = inputs.shape
    n_dp, n_row, n_col = (lax.axis_size(name) for name in ("dp", "row", "col"))
    voxels = planes * tile_x * tile_y
    extended = voxels + 2 * HALO * tile_x * tile_y
    width, channels = up_weight.shape
    share = width // (n_dp * n_row)
    bf16, f32 = jnp.bfloat16, jnp.float32
    dma = pltpu.SemaphoreType.DMA
    taps = kernel.shape[0]
    tap_rows = -(-taps // 16) * 16
    vmem, anywhere = pl.BlockSpec(memory_space=pltpu.VMEM), pl.BlockSpec(memory_space=pl.ANY)
    outs = pl.pallas_call(
        functools.partial(block_kernel, (planes, tile_x, tile_y, n_dp, n_row, n_col)),
        out_shape=(
            jax.ShapeDtypeStruct((voxels, local), bf16),
            jax.ShapeDtypeStruct((voxels, local), bf16),
            jax.ShapeDtypeStruct((share, channels), bf16),
            jax.ShapeDtypeStruct((share, channels), bf16),
            jax.ShapeDtypeStruct((taps, channels), f32),
        ),
        in_specs=[anywhere] * 5,
        out_specs=(vmem,) * 5,
        scratch_shapes=[
            pltpu.VMEM(kernel.shape, f32),
            pltpu.VMEM((voxels, width), bf16),
            pltpu.VMEM((voxels, width), bf16),
            pltpu.VMEM((width, channels), bf16),
            pltpu.VMEM((width, channels), bf16),
            pltpu.VMEM((extended, channels), bf16),
            pltpu.VMEM((extended, channels), bf16),
            pltpu.VMEM((voxels, channels), f32),
            pltpu.VMEM((voxels, channels), bf16),
            pltpu.VMEM((voxels, channels), bf16),
            pltpu.VMEM((tile_y // 8, planes + 2 * HALO, tile_x, 24, LANES), f32),
            pltpu.VMEM((planes * tile_x, tile_y, LANES), f32),
            pltpu.VMEM((2, n_col, voxels, local), bf16),
            pltpu.VMEM((2, n_col, voxels, local), bf16),
            pltpu.VMEM((2, width, voxels), bf16),
            pltpu.VMEM((2, n_col // 2, local, channels), bf16),
            pltpu.VMEM((2, n_col // 2, local, channels), bf16),
            pltpu.VMEM((2, width // 2, channels), bf16),
            pltpu.VMEM((2, n_row, share, channels), bf16),
            pltpu.VMEM((tap_rows, channels), f32),
            pltpu.VMEM((tap_rows, channels), bf16),
            pltpu.VMEM((tap_rows, channels), bf16),
            pltpu.VMEM((tap_rows, channels // 2), bf16),
            pltpu.VMEM((n_row, tap_rows, channels // 2), bf16),
            pltpu.VMEM((tap_rows, channels // 2), f32),
            pltpu.VMEM((tap_rows, channels // 2), f32),
            dma((5,)),
            dma((2, 2, n_col)), dma((2, 2, n_col)),
            dma((2, 2)), dma((2, 2)),
            dma((2, n_col)), dma((2, n_col)),
            dma((2, n_col // 2)), dma((2, n_col // 2)),
            dma((2, n_row)), dma((2, n_row)),
            dma((n_row + 1,)), dma((n_row + 1,)),
        ],
        compiler_params=pltpu.CompilerParams(
            collective_id=0, has_side_effects=True, vmem_limit_bytes=56 << 20
        ),
    )(inputs.reshape(voxels, local), cotangent.reshape(voxels, local), up_weight, down_weight, kernel)
    outs = pl.pallas_call(
        hand_on,
        out_shape=tuple(jax.ShapeDtypeStruct(out.shape, out.dtype) for out in outs),
        in_specs=[anywhere] * 5,
        out_specs=(anywhere,) * 5,
        scratch_shapes=[dma((5,))],
    )(*outs)
    return (outs[0].reshape(inputs.shape), outs[1].reshape(inputs.shape)) + tuple(outs[2:])


def solution(mesh):
    placed = (
        P("dp", "row", None, None, "col"),
        P(None, "col"),
        P(None, "col"),
        P(None, "col"),
        P("dp", "row", None, None, "col"),
    )
    return jax.shard_map(
        on_device,
        mesh=mesh,
        in_specs=placed,
        out_specs=(
            P("dp", "row", None, None, "col"),
            P("dp", "row", None, None, "col"),
            P(("dp", "row"), "col"),
            P(("dp", "row"), "col"),
            P(None, "col"),
        ),
        check_vma=False,
    )
```

```python
import functools

import jax
import jax.numpy as jnp
from jax import lax
from jax.experimental import pallas as pl
from jax.experimental.pallas import tpu as pltpu
from jax.sharding import PartitionSpec as P

LANES = 128
HALO = 2


def aligned(index, size):
    return pl.ds(pl.multiple_of(index * size, size), size)


def clear_windows(win):
    halves, depth, tile_x, _, lanes = win.shape
    zeros = jnp.zeros((8, lanes), jnp.float32)
    for z in range(depth):
        for x in range(tile_x):
            win[0, z, x, 0:8] = zeros
            win[halves - 1, z, x, 16:24] = zeros


def fill_windows(win, field, cols):
    halves, depth, tile_x, _, _ = win.shape
    tile_y = 8 * halves
    for z in range(depth):
        for x in range(tile_x):
            first_row = (z * tile_x + x) * tile_y
            line = field[first_row : first_row + tile_y, cols].astype(jnp.float32)
            for h in range(halves):
                for part in range(3):
                    first = 8 * (h + part - 1)
                    if 0 <= first < tile_y:
                        win[h, z, x, 8 * part : 8 * part + 8] = line[first : first + 8]


def pairs(source_z, source_x, planes, tile_x):
    for a in range(5):
        z = source_z - a
        if 0 <= z < planes:
            for b in range(5):
                x = source_x - b + 2
                if 0 <= x < tile_x:
                    yield a, b, z, x


def stencil_half(win, half, kernel, cols, mirror, planes, tile_x):
    accs = [[None] * tile_x for _ in range(planes)]
    for c in range(5):
        taps = {}
        for a in range(5):
            for b in range(5):
                t = 25 * a + 5 * b + c
                t = 124 - t if mirror else t
                taps[a, b] = jnp.broadcast_to(kernel[t : t + 1, cols], (8, LANES))
        for sz in range(planes + 2 * HALO):
            for sx in range(tile_x):
                cells = win[half, sz, sx, 6 + c : 14 + c]
                for a, b, z, x in pairs(sz, sx, planes, tile_x):
                    term = taps[a, b] * cells
                    accs[z][x] = term if accs[z][x] is None else accs[z][x] + term
    return accs


def stencil(win, field, kernel, mirror, planes, tile_x, wide, finish, midway=None):
    halves = win.shape[0]
    tile_y = 8 * halves

    @pl.loop(0, kernel.shape[1] // LANES)
    def _(block):
        cols = aligned(block, LANES)
        fill_windows(win, field, cols)
        if midway is not None:
            pl.when(block == kernel.shape[1] // LANES // 2)(midway)

        @pl.loop(0, halves)
        def _(half):
            accs = stencil_half(win, half, kernel, cols, mirror, planes, tile_x)
            for z in range(planes):
                for x in range(tile_x):
                    first = (z * tile_x + x) * tile_y + half * 8
                    wide[pl.ds(pl.multiple_of(first, 8), 8), cols] = accs[z][x]

        for line in range(planes * tile_x):
            rows = slice(line * tile_y, (line + 1) * tile_y)
            finish(rows, cols, wide[rows, cols])


def tap_sums(win, tmp, field, grad, out, planes, tile_x):
    halves = win.shape[0]
    tile_y = 8 * halves
    first_row = HALO * tile_x * tile_y

    @pl.loop(0, out.shape[1] // LANES)
    def _(block):
        cols = aligned(block, LANES)
        fill_windows(win, field, cols)
        for line in range(planes * tile_x):
            rows = slice(first_row + line * tile_y, first_row + (line + 1) * tile_y)
            tmp[line] = grad[rows, cols].astype(jnp.float32)
        for c in range(5):
            def one_half(half, sums):
                sums = list(sums)
                rows = aligned(half, 8)
                grads = [tmp[line, rows, :] for line in range(planes * tile_x)]
                for sz in range(planes + 2 * HALO):
                    for sx in range(tile_x):
                        cells = win[half, sz, sx, 6 + c : 14 + c]
                        for a, b, z, x in pairs(sz, sx, planes, tile_x):
                            sums[5 * a + b] = sums[5 * a + b] + cells * grads[z * tile_x + x]
                return tuple(sums)

            sums = lax.fori_loop(0, halves, one_half, (jnp.zeros((8, LANES), jnp.float32),) * 25)
            for ab in range(25):
                t = 5 * ab + c
                out[t : t + 1, cols] = jnp.sum(sums[ab], axis=0, keepdims=True)


def block_kernel(
    sizes, inputs, cotangent, up_weight, down_weight, stencil_weights,
    block_output, input_grad, up_grad, down_grad, kernel_grad,
    kernel, xg, cg, upw, dnw, hid, grd, wide, act, hgr, win, tmp, sent, got, turned,
    first_out, first_in, second_out, second_in, taps, taps_out, taps_in, share_out, share_in, half_out, half_in,
    load_sem, ag_s, ag_r, halo_s, halo_r, rs_s, rs_r, pair_s, pair_r, row_s, row_r, kg_s, kg_r,
):
    planes, tile_x, tile_y, n_dp, n_row, n_col = sizes
    dp, row, col = lax.axis_index("dp"), lax.axis_index("row"), lax.axis_index("col")
    partner = {"dp": 1 - dp}
    voxels, local = inputs.shape
    channels = kernel.shape[1]
    plane = tile_x * tile_y
    own = slice(HALO * plane, HALO * plane + voxels)
    tile = min(256, channels)
    wtile = min(256, local)
    n_half = n_col // 2
    share = first_out.shape[1] * local // n_row
    bf16, f32 = jnp.bfloat16, jnp.float32
    mine = aligned(col, local)

    loads = [
        pltpu.make_async_copy(source, target, load_sem.at[i])
        for i, (source, target) in enumerate(
            ((inputs, xg.at[:, mine]), (up_weight, upw), (stencil_weights, kernel), (cotangent, cg.at[:, mine]), (down_weight, dnw))
        )
    ]
    for load in loads:
        load.start()

    barrier = pltpu.get_barrier_semaphore()

    @pl.loop(1, n_col)
    def _(k):
        pl.semaphore_signal(barrier, inc=1, device_id={"col": lax.rem(col + k, n_col)})

    @pl.loop(1, n_row)
    def _(k):
        pl.semaphore_signal(barrier, inc=1, device_id={"row": lax.rem(row + k, n_row)})

    pl.semaphore_signal(barrier, inc=1, device_id=partner)
    pl.semaphore_wait(barrier, n_col + n_row - 1)

    def remote(source, target, send, receive, device):
        return pltpu.make_async_remote_copy(
            src_ref=source, dst_ref=target, send_sem=send, recv_sem=receive,
            device_id=device, device_id_type=pl.DeviceIdType.MESH,
        )

    def hop(i, side, step):
        gathered = (xg, cg)[i]
        source = (inputs, cotangent)[i] if step == 0 else gathered.at[:, aligned(col - side * step, local)]
        return remote(
            source, gathered.at[:, aligned(col - side * step, local)],
            ag_s.at[i, (side + 1) // 2, step], ag_r.at[i, (side + 1) // 2, step], {"col": col + side},
        )

    def inside(index):
        return jnp.logical_and(index >= 0, index < n_col)

    def hop_start(i, step):
        for side in (1, -1):
            pl.when(jnp.logical_and(inside(col + side), inside(col - side * step)))(hop(i, side, step).start)

    def hop_received(i, step):
        for side in (1, -1):
            pl.when(inside(col - side * (step + 1)))(hop(i, side, step).wait_recv)

    def hop_sent(i, step):
        for side in (1, -1):
            pl.when(jnp.logical_and(inside(col + side), inside(col - side * step)))(hop(i, side, step).wait_send)

    def advance(i, step):
        if step < n_col - 1:
            hop_received(i, step - 1)
            hop_start(i, step)

    def each(count, action, first=1):
        @pl.loop(first, count)
        def _(k):
            action(k)

    hop_start(0, 0)
    clear_windows(win)
    for step in range(1, n_col - 1):
        advance(0, step)
    hop_start(1, 0)
    hop_received(0, n_col - 2)
    loads[0].wait()
    loads[1].wait()

    @pl.loop(0, channels // tile)
    def _(n):
        cols = aligned(n, tile)
        hid[own, cols] = jnp.dot(xg[...], upw[:, cols], preferred_element_type=f32).astype(bf16)

    def turn(i, left):
        @pl.loop(0, n_col)
        def _(chunk):
            turned[i, aligned(chunk, local)] = left[:, aligned(chunk, local)].T

    def halo(i, field, side):
        if side:
            source, target, peer = field.at[HALO * plane : 2 * HALO * plane], voxels + HALO * plane, row - 1
        else:
            source, target, peer = field.at[voxels : voxels + HALO * plane], 0, row + 1
        return remote(
            source, field.at[target : target + HALO * plane], halo_s.at[i, side], halo_r.at[i, side], {"row": peer}
        )

    def halo_start(i, field):
        @pl.when(row < n_row - 1)
        def _():
            halo(i, field, 0).start()

        @pl.when(row > 0)
        def _():
            halo(i, field, 1).start()

        @pl.when(row == 0)
        def _():
            field[0 : HALO * plane] = jnp.zeros((HALO * plane, channels), bf16)

        @pl.when(row == n_row - 1)
        def _():
            field[voxels + HALO * plane :] = jnp.zeros((HALO * plane, channels), bf16)

    def halo_wait(i, field):
        @pl.when(row > 0)
        def _():
            halo(i, field, 0).wait_recv()
            halo(i, field, 1).wait_send()

        @pl.when(row < n_row - 1)
        def _():
            halo(i, field, 1).wait_recv()
            halo(i, field, 0).wait_send()

    halo_start(0, hid)
    advance(1, 1)
    turn(0, xg)
    loads[2].wait()
    halo_wait(0, hid)

    def activate(rows, cols, preact):
        act[rows, cols] = (preact * jax.nn.sigmoid(preact)).astype(bf16)

    stencil(win, hid, kernel, False, planes, tile_x, wide, activate, lambda: advance(1, 2))

    loads[3].wait()
    loads[4].wait()
    for step in range(3, n_col - 1):
        advance(1, step)
    hop_received(1, n_col - 2)

    @pl.loop(0, channels // tile)
    def _(n):
        cols = aligned(n, tile)
        act_grad = jnp.dot(cg[...], dnw[:, cols], preferred_element_type=f32)
        preact = wide[:, cols]
        logistic = jax.nn.sigmoid(preact)
        grd[own, cols] = (act_grad * logistic * (1.0 + preact * (1.0 - logistic))).astype(bf16)

    halo_start(1, grd)

    def pair(i, j):
        return remote(first_out.at[i, j], first_in.at[i, j], pair_s.at[i, j], pair_r.at[i, j], partner)

    def grad_for_partner(i, right):
        @pl.loop(0, n_half)
        def _(j):
            chunk = aligned((1 - dp) * n_half + j, local)

            @pl.loop(0, channels // tile)
            def _(n):
                cols = aligned(n, tile)
                first_out[i, j, :, cols] = jnp.dot(
                    turned[1 - i, chunk], right[:, cols], preferred_element_type=f32
                ).astype(bf16)

            pair(i, j).start()

    def row_copy(i, k):
        peer = lax.rem(row + k, n_row)
        return remote(
            second_out.at[i, aligned(peer, share)], second_in.at[i, k], row_s.at[i, k], row_r.at[i, k], {"row": peer}
        )

    def grad_own(i, right):
        @pl.loop(0, n_half)
        def _(j):
            chunk = aligned(dp * n_half + j, local)
            pair(i, j).wait_recv()

            @pl.loop(0, channels // tile)
            def _(n):
                cols = aligned(n, tile)
                product = jnp.dot(turned[1 - i, chunk], right[:, cols], preferred_element_type=f32).astype(bf16)
                both = product.astype(f32) + first_in[i, j, :, cols].astype(f32)
                second_out[i, aligned(j, local), cols] = both.astype(bf16)

            for part in range(local // share):
                peer = j * (local // share) + part
                k = lax.rem(peer - row + n_row, n_row)
                pl.when(peer != row)(lambda: row_copy(i, k).start())

    def grad_finish(i, out):
        each(n_row, lambda k: row_copy(i, k).wait_recv())

        @pl.loop(0, channels // tile)
        def _(n):
            cols = aligned(n, tile)
            total = second_out[i, aligned(row, share), cols].astype(f32)
            for k in range(1, n_row):
                total = total + second_in[i, k, :, cols].astype(f32)
            out[:, cols] = total.astype(bf16)

        each(n_row, lambda k: row_copy(i, k).wait_send())
        each(n_half, lambda j: pair(i, j).wait_send(), 0)

    def column_copy(i, k):
        return remote(sent.at[i, k], got.at[i, k], rs_s.at[i, k], rs_r.at[i, k], {"col": lax.rem(col + k, n_col)})

    def column_partials(i, left, weight):
        def one(k):
            first = lax.rem(col + k, n_col) * local

            @pl.loop(0, local // wtile)
            def _(n):
                rows = pl.ds(pl.multiple_of(first + n * wtile, wtile), wtile)
                product = lax.dot_general(
                    left[...], weight[rows, :], (((1,), (1,)), ((), ())), preferred_element_type=f32
                )
                sent[i, k, :, aligned(n, wtile)] = product.astype(bf16)

        @pl.loop(1, n_col)
        def _(k):
            one(k)
            column_copy(i, k).start()

        one(0)

    def column_finish(i, residual, out):
        each(n_col, lambda k: column_copy(i, k).wait_recv())
        total = sent[i, 0].astype(f32)
        for k in range(1, n_col):
            total = total + got[i, k].astype(f32)
        out[...] = (residual[:, mine].astype(f32) + total).astype(bf16)
        each(n_col, lambda k: column_copy(i, k).wait_send())

    turn(1, cg)
    grad_for_partner(0, act)
    column_partials(0, act, dnw)
    grad_own(0, act)
    halo_wait(1, grd)

    def keep(rows, cols, total):
        hgr[rows, cols] = total.astype(bf16)

    stencil(win, grd, kernel, True, planes, tile_x, wide, keep)
    grad_for_partner(1, hgr)
    column_partials(1, hgr, upw)
    grad_own(1, hgr)
    tap_sums(win, tmp, hid, grd, taps, planes, tile_x)
    taps_out[0 : kernel.shape[0]] = taps[0 : kernel.shape[0]].astype(bf16)
    taps_out[kernel.shape[0] :] = jnp.zeros((taps_out.shape[0] - kernel.shape[0], channels), bf16)
    whole_taps = remote(taps_out, taps_in, kg_s.at[0], kg_r.at[0], partner)
    whole_taps.start()
    column_finish(0, xg, block_output)
    whole_taps.wait_recv()
    some = aligned(dp, channels // 2)
    share_out[...] = (taps_out[:, some].astype(f32) + taps_in[:, some].astype(f32)).astype(bf16)

    def taps_copy(k):
        return remote(share_out, share_in.at[k], kg_s.at[k], kg_r.at[k], {"row": lax.rem(row + k, n_row)})

    each(n_row, lambda k: taps_copy(k).start())
    grad_finish(0, down_grad)
    column_finish(1, cg, input_grad)
    each(n_row, lambda k: taps_copy(k).wait_recv())
    total = share_out[...].astype(f32)
    for k in range(1, n_row):
        total = total + share_in[k].astype(f32)
    half_out[...] = total
    halves = remote(half_out, half_in, kg_s.at[n_row], kg_r.at[n_row], partner)
    halves.start()
    kernel_grad[:, some] = half_out[0 : kernel.shape[0]]
    grad_finish(1, up_grad)
    halves.wait_recv()
    kernel_grad[:, aligned(1 - dp, channels // 2)] = half_in[0 : kernel.shape[0]]
    for i in range(2):
        for step in range(n_col - 1):
            hop_sent(i, step)
    whole_taps.wait_send()
    each(n_row, lambda k: taps_copy(k).wait_send())
    halves.wait_send()


def hand_on(*refs):
    arrived, done = refs[15], refs[16]
    fetches = [pltpu.make_async_copy(refs[i], refs[10 + i], arrived.at[i]) for i in range(5)]
    stores = [pltpu.make_async_copy(refs[10 + i], refs[5 + i], done.at[i]) for i in range(5)]
    for fetch in fetches:
        fetch.start()
    for fetch, store in zip(fetches, stores):
        fetch.wait()
        store.start()
    for store in stores:
        store.wait()


def on_device(inputs, up_weight, down_weight, kernel, cotangent):
    _, planes, tile_x, tile_y, local = inputs.shape
    n_dp, n_row, n_col = (lax.axis_size(name) for name in ("dp", "row", "col"))
    voxels = planes * tile_x * tile_y
    extended = voxels + 2 * HALO * tile_x * tile_y
    width, channels = up_weight.shape
    share = width // (n_dp * n_row)
    bf16, f32 = jnp.bfloat16, jnp.float32
    dma = pltpu.SemaphoreType.DMA
    taps = kernel.shape[0]
    tap_rows = -(-taps // 16) * 16
    vmem, anywhere = pl.BlockSpec(memory_space=pltpu.VMEM), pl.BlockSpec(memory_space=pl.ANY)
    outs = pl.pallas_call(
        functools.partial(block_kernel, (planes, tile_x, tile_y, n_dp, n_row, n_col)),
        out_shape=(
            jax.ShapeDtypeStruct((voxels, local), bf16),
            jax.ShapeDtypeStruct((voxels, local), bf16),
            jax.ShapeDtypeStruct((share, channels), bf16),
            jax.ShapeDtypeStruct((share, channels), bf16),
            jax.ShapeDtypeStruct((taps, channels), f32),
        ),
        in_specs=[anywhere] * 5,
        out_specs=(vmem,) * 5,
        scratch_shapes=[
            pltpu.VMEM(kernel.shape, f32),
            pltpu.VMEM((voxels, width), bf16),
            pltpu.VMEM((voxels, width), bf16),
            pltpu.VMEM((width, channels), bf16),
            pltpu.VMEM((width, channels), bf16),
            pltpu.VMEM((extended, channels), bf16),
            pltpu.VMEM((extended, channels), bf16),
            pltpu.VMEM((voxels, channels), f32),
            pltpu.VMEM((voxels, channels), bf16),
            pltpu.VMEM((voxels, channels), bf16),
            pltpu.VMEM((tile_y // 8, planes + 2 * HALO, tile_x, 24, LANES), f32),
            pltpu.VMEM((planes * tile_x, tile_y, LANES), f32),
            pltpu.VMEM((2, n_col, voxels, local), bf16),
            pltpu.VMEM((2, n_col, voxels, local), bf16),
            pltpu.VMEM((2, width, voxels), bf16),
            pltpu.VMEM((2, n_col // 2, local, channels), bf16),
            pltpu.VMEM((2, n_col // 2, local, channels), bf16),
            pltpu.VMEM((2, width // 2, channels), bf16),
            pltpu.VMEM((2, n_row, share, channels), bf16),
            pltpu.VMEM((tap_rows, channels), f32),
            pltpu.VMEM((tap_rows, channels), bf16),
            pltpu.VMEM((tap_rows, channels), bf16),
            pltpu.VMEM((tap_rows, channels // 2), bf16),
            pltpu.VMEM((n_row, tap_rows, channels // 2), bf16),
            pltpu.VMEM((tap_rows, channels // 2), f32),
            pltpu.VMEM((tap_rows, channels // 2), f32),
            dma((5,)),
            dma((2, 2, n_col)), dma((2, 2, n_col)),
            dma((2, 2)), dma((2, 2)),
            dma((2, n_col)), dma((2, n_col)),
            dma((2, n_col // 2)), dma((2, n_col // 2)),
            dma((2, n_row)), dma((2, n_row)),
            dma((n_row + 1,)), dma((n_row + 1,)),
        ],
        compiler_params=pltpu.CompilerParams(
            collective_id=0, has_side_effects=True, vmem_limit_bytes=56 << 20
        ),
    )(inputs.reshape(voxels, local), cotangent.reshape(voxels, local), up_weight, down_weight, kernel)
    outs = pl.pallas_call(
        hand_on,
        out_shape=tuple(jax.ShapeDtypeStruct(out.shape, out.dtype) for out in outs),
        in_specs=[anywhere] * 5,
        out_specs=(anywhere,) * 5,
        scratch_shapes=[pltpu.VMEM(out.shape, out.dtype) for out in outs] + [dma((5,)), dma((5,))],
    )(*outs)
    return (outs[0].reshape(inputs.shape), outs[1].reshape(inputs.shape)) + tuple(outs[2:])


def solution(mesh):
    placed = (
        P("dp", "row", None, None, "col"),
        P(None, "col"),
        P(None, "col"),
        P(None, "col"),
        P("dp", "row", None, None, "col"),
    )
    return jax.shard_map(
        on_device,
        mesh=mesh,
        in_specs=placed,
        out_specs=(
            P("dp", "row", None, None, "col"),
            P("dp", "row", None, None, "col"),
            P(("dp", "row"), "col"),
            P(("dp", "row"), "col"),
            P(None, "col"),
        ),
        check_vma=False,
    )
```
